256 devices in a mesh: dp: 2 (over y_lo), ulysses: 8 (over x, core), blk: 16 (over y_hi, z).
Axes of the slice: x: 4, y: 4 (y_hi: 2, y_lo: 2; y = y_hi * 2 + y_lo), z: 8, core: 2. Of those that a mesh axis runs over, the one named last changes fastest.
Arguments:
- hidden_in: bfloat16 [2, 16384, 4096], P('dp', ('blk', 'ulysses')), may hold values from -6 to 6
- queries: bfloat16 [2, 16384, 2048], P('dp', ('blk', 'ulysses')), may hold values from -240 to 240
- pair_weight: bfloat16 [4096, 2048], P(('dp', 'blk')), may hold values from -0.09375 to 0.09375
- span_order: int32 [2, 32], P('dp'), may hold values from 0 to 31, each once within a row
- yarn_divisor: int32 [64], replicated, may hold values from 1 to 8
Outputs:
- attended: bfloat16 [2, 16384, 2048], P('dp', ('blk', 'ulysses'))
The draws below stay inside these ranges and needn't reach their ends.
All inputs are finite; a program needn't handle non-finite values.
Results may differ from the reference program's by a relative error of at most 0.02.
The reference program's roundings to bfloat16 on the way count: a program that leaves them out, or rounds other values in their place, can miss the bound.
Values may be sent and summed in bfloat16 or wider, within the bound.
A program may use at most 128 MiB of HBM per device.

```python
import math
import jax
import jax.numpy as jnp
from jax import lax

D = 4096
KVH = 8
HD = 128
QH = 16
STEPS = 3
SEQS = 2
BLOCKS = 16
BLOCK = 1024
SPAN = 512
SEQ = 16384


def draw_queries(key, part):
    first_key, second_key, third_key = jax.random.split(key, 3)
    shape_full = (SEQS, SEQ, QH, HD)
    base_values = jnp.clip(jax.random.normal(first_key, shape_full, jnp.float32), -4.0, 4.0)
    picked = jax.random.randint(second_key, (SEQS, SEQ, QH, 1), 0, 64) == 0
    boost = jnp.exp(jax.random.uniform(third_key, (SEQS, SEQ, QH, 1), jnp.float32, math.log(30.0), math.log(60.0)))
    scaled = base_values * jnp.where(picked, boost, 1.0)
    return scaled.reshape(SEQS, SEQ, QH * HD).astype(jnp.bfloat16)


def with_ends(entries, rng, low, top_value):
    place = [jax.random.randint(jax.random.fold_in(rng, axis), (), 0, length) for axis, length in enumerate(entries.shape)]
    longest = entries.shape.index(max(entries.shape))
    neighbour = place[:longest] + [(place[longest] + 1) % entries.shape[longest]] + place[longest + 1:]
    return entries.at[tuple(place)].set(low).at[tuple(neighbour)].set(top_value)


def block_levels(stream_key, extent, pieces, least, high):
    level = 1.0
    for dim, shards_of in pieces:
        heights = jax.random.uniform(jax.random.fold_in(jax.random.fold_in(stream_key, 6), dim), (shards_of,), jnp.float32, least / len(pieces), high / len(pieces))
        level = level * jnp.repeat(jnp.exp(heights), extent[dim] // shards_of).reshape((-1,) + (1,) * (len(extent) - 1 - dim))
    return level


def scatter_about(own_key, dims, width, bound, cuts=(), kind=jnp.bfloat16):
    entries = width * jax.random.normal(own_key, dims, jnp.float32)
    if cuts:
        entries = entries * block_levels(own_key, dims, cuts, -0.22, 0.18)
    return jnp.clip(entries, -bound, bound).astype(kind)


def setup_inputs(seed: int = 0) -> dict:
    arg_keys = jax.random.split(jax.random.key(seed), 6)
    hidden_in = scatter_about(arg_keys[0], (SEQS, SEQ, D), 1.0, 6.0, ((0, 2), (1, 128)))
    queries = draw_queries(jax.random.fold_in(arg_keys[5], 71), 0)
    pair_weight = scatter_about(arg_keys[2], (D, 2 * KVH * HD), D ** -0.5, 0.09375, ((0, 32),))
    span_order = jax.vmap(lambda own: jax.random.permutation(own, 2 * BLOCKS))(jax.random.split(arg_keys[3], SEQS)).reshape((SEQS, 2 * BLOCKS)).astype(jnp.int32)
    yarn_divisor = with_ends(jax.random.randint(arg_keys[4], (HD // 2,), 1, 9), jax.random.fold_in(arg_keys[4], 1), 1, 8).astype(jnp.int32)
    return dict(hidden_in=hidden_in, queries=queries, pair_weight=pair_weight, span_order=span_order, yarn_divisor=yarn_divisor)


LOG_BASE = math.log(500000.0)

def rotate(vectors, angle_table):
    half_dim = vectors.shape[-1] // 2
    first_half = vectors[..., :half_dim]
    second_half = vectors[..., half_dim:]
    cosine = jnp.cos(angle_table)
    sine_part = jnp.sin(angle_table)
    return jnp.concatenate([first_half * cosine - second_half * sine_part, second_half * cosine + first_half * sine_part], axis=-1)

def angles(positions, yarn_divisor):
    half_dim = yarn_divisor.shape[0]
    scaled = 2.0 * jnp.arange(half_dim, dtype=jnp.float32) / (2 * half_dim)
    inverse = jnp.exp(-LOG_BASE * scaled) / yarn_divisor.astype(jnp.float32)
    return positions.astype(jnp.float32)[:, None] * inverse[None, :]

def reference(hidden_in, queries, pair_weight, span_order, yarn_divisor):
    score_scale = 1.0 / math.sqrt(HD)
    group_size = QH // KVH
    kv_width = KVH * HD
    rows_all = jnp.arange(SEQ, dtype=jnp.int32)
    results = []
    for sequence in range(SEQS):
        positions = (span_order[sequence][rows_all // SPAN] * SPAN + rows_all % SPAN).astype(jnp.int32)
        angle_table = angles(positions, yarn_divisor)[:, None, :]
        projected = jnp.dot(hidden_in[sequence], pair_weight, preferred_element_type=jnp.float32)
        keys = rotate(projected[:, :kv_width].reshape(SEQ, KVH, HD), angle_table).astype(jnp.bfloat16)
        values = projected[:, kv_width:].astype(jnp.bfloat16).reshape(SEQ, KVH, HD)
        rotated = rotate(queries[sequence].astype(jnp.float32).reshape(SEQ, QH, HD), angle_table).astype(jnp.bfloat16)
        keys_by_head = keys.transpose(1, 0, 2)
        values_by_head = values.transpose(1, 0, 2)

        def one_head(flat_index):
            block_index = (flat_index // QH).astype(jnp.int32)
            head_index = (flat_index % QH).astype(jnp.int32)
            kv_head = (head_index // group_size).astype(jnp.int32)
            row_start = (block_index * BLOCK).astype(jnp.int32)
            query_rows = lax.dynamic_slice(rotated, (row_start, head_index, jnp.int32(0)), (BLOCK, 1, HD))[:, 0, :]
            query_pos = lax.dynamic_slice(positions, (row_start,), (BLOCK,))
            source_blocks = (block_index - jnp.arange(STEPS + 1, dtype=jnp.int32)) % BLOCKS
            key_index = (source_blocks[:, None] * BLOCK + jnp.arange(BLOCK, dtype=jnp.int32)[None, :]).reshape(-1).astype(jnp.int32)
            key_rows = lax.dynamic_index_in_dim(keys_by_head, kv_head, 0, False)[key_index]
            value_rows = lax.dynamic_index_in_dim(values_by_head, kv_head, 0, False)[key_index]
            key_pos = positions[key_index]
            score = jnp.dot(query_rows, key_rows.T, preferred_element_type=jnp.float32) * score_scale
            allowed = key_pos[None, :] <= query_pos[:, None]
            row_top = lax.optimization_barrier(jnp.max(jnp.where(allowed, score, -jnp.inf), axis=1))
            weights = jnp.where(allowed, jnp.exp(score - row_top[:, None]), 0.0)
            denominator = lax.optimization_barrier(jnp.sum(weights, axis=1))
            numerator = jnp.dot(weights.astype(jnp.bfloat16), value_rows, preferred_element_type=jnp.float32)
            return (numerator / denominator[:, None]).astype(jnp.bfloat16)
        attended_heads = lax.map(one_head, jnp.arange(BLOCKS * QH, dtype=jnp.int32))
        attended_heads = attended_heads.reshape(BLOCKS, QH, BLOCK, HD).transpose(0, 2, 1, 3).reshape(SEQ, QH * HD)
        results.append(attended_heads)
    return jnp.stack(results)
```

```python
import math

import jax
import jax.numpy as jnp
from jax import lax
from jax.experimental import pallas as pl
from jax.experimental.pallas import tpu as pltpu
from jax.sharding import PartitionSpec as P

KVH = 8
HD = 128
QH = 16
STEPS = 3
UL = 8
NZ = 8
LOG_BASE = math.log(500000.0)
MESH = pl.DeviceIdType.MESH
SCALE2 = (1.0 / math.sqrt(HD)) * math.log2(math.e)
NEG = -1.0e30
FAR = 2.0e30


def wrap(value, size):
    return lax.rem(value + size, size)


def kernel(
    order_ref, hid, qry, pw, cos_ref, sin_ref, out,
    wbuf, hbuf, qbuf, qrot, kvbuf, m_ref, l_ref, acc_ref, obuf,
    ssem, rsem, lsem,
):
    dp = lax.axis_index("dp")
    u = lax.axis_index("ulysses")
    blk = lax.axis_index("blk")
    core = lax.rem(u, 2)
    x = u // 2
    yh = blk // NZ
    z = lax.rem(blk, NZ)
    y = yh * 2 + dp

    counter = [0]

    def take(n):
        base = counter[0]
        counter[0] += n
        return base

    def ul(index):
        return {"ulysses": index}

    def ydev(offset):
        other = lax.rem(y + offset, 4)
        return other, {"dp": lax.rem(other, 2), "blk": (other // 2) * NZ + z}

    def zdev(offset):
        return {"blk": yh * NZ + wrap(z + offset, NZ)}

    u_plus, u_minus = lax.rem(u + 2, UL), lax.rem(u + UL - 2, UL)
    u_far = lax.rem(u + 4, UL)
    partner = u + 1 - 2 * core
    next_blk = {"blk": lax.rem(blk + 1, 16)}
    prev_blk = {"blk": lax.rem(blk + 15, 16)}

    def rcopy(src, dst, index, device):
        return pltpu.make_async_remote_copy(
            src_ref=src, dst_ref=dst, send_sem=ssem.at[index], recv_sem=rsem.at[index],
            device_id=device, device_id_type=MESH,
        )

    sends = []

    def send(src, dst, index, device):
        copy = rcopy(src, dst, index, device)
        copy.start()
        sends.append(copy)

    def arrive(dst, index):
        rcopy(dst, dst, index, ul(partner)).wait_recv()

    barrier = pltpu.get_barrier_semaphore()
    greet = [ul(lax.rem(u + o, UL)) for o in range(1, UL)]
    greet += [ydev(o)[1] for o in range(1, 4)]
    greet += [zdev(1), zdev(-1), next_blk, prev_blk]
    for device in greet:
        pl.semaphore_signal(barrier, inc=1, device_id=device, device_id_type=MESH)
    pl.semaphore_wait(barrier, len(greet))

    own_k = pw.at[:, pl.ds(pl.multiple_of(u * HD, HD), HD)]
    own_v = pw.at[:, pl.ds(pl.multiple_of(KVH * HD + u * HD, HD), HD)]
    WB = (take(4), take(3))
    WAY = take(3)
    WAZ = (take(8), take(6))
    WBY = take(4)
    HX, HR, HP = take(4), take(2), take(7)
    QX = take(7)
    KV = take(12)
    OX = take(7)

    def vpiece(yy, zz):
        return wbuf.at[lax.rem(yy, 2), yy // 2, zz, :, pl.ds(HD, HD)]

    def kpiece(yy, zz):
        return wbuf.at[lax.rem(yy, 2), yy // 2, zz, :, pl.ds(0, HD)]

    def kbundle(g, zz):
        return wbuf.at[g, :, zz, :, pl.ds(0, HD)]

    def vbundle(yy, lo, size):
        return wbuf.at[lax.rem(yy, 2), yy // 2, pl.ds(lo, size), :, pl.ds(HD, HD)]

    send(own_v, vpiece(y, z), WB[0], zdev(1))
    send(own_v, vpiece(y, z), WB[1], zdev(-1))
    for o in range(1, 4):
        send(own_k, kpiece(y, z), WAY + o - 1, ydev(o)[1])

    local = [
        pltpu.make_async_copy(own_k, kpiece(y, z), lsem.at[0]),
        pltpu.make_async_copy(own_v, vpiece(y, z), lsem.at[1]),
        pltpu.make_async_copy(hid, hbuf.at[u], lsem.at[2]),
        pltpu.make_async_copy(
            qry.at[:, pl.ds(pl.multiple_of(u * 2 * HD, HD), 2 * HD)], qbuf.at[u], lsem.at[3]
        ),
    ]
    for copy in local:
        copy.start()

    send(hid, hbuf.at[u], HP, ul(partner))
    for half in range(2):
        rows = pl.ds(half * 64, 64)
        send(hid.at[rows], hbuf.at[u, rows], HX + half, ul(u_plus))
        send(hid.at[rows], hbuf.at[u, rows], HX + 2 + half, ul(u_minus))
    for o in range(1, UL):
        peer = lax.rem(u + o, UL)
        send(
            qry.at[:, pl.ds(pl.multiple_of(peer * 2 * HD, HD), 2 * HD)],
            qbuf.at[u], QX + o - 1, ul(peer),
        )

    hops = (4, 3)
    steps = (-1, 1)

    def v_hop(h):
        for way in range(2):
            if h <= hops[way]:
                zz = wrap(z + steps[way] * h, NZ)
                arrive(vpiece(y, zz), WB[way] + h - 1)
                if h < hops[way]:
                    send(vpiece(y, zz), vpiece(y, zz), WB[way] + h, zdev(-steps[way]))

    def k_hop(h):
        for way in range(2):
            for g in range(2):
                if h == 0 or h <= hops[way]:
                    zz = wrap(z + steps[way] * h, NZ)
                    if h > 0:
                        arrive(kbundle(g, zz), WAZ[way] + 2 * (h - 1) + g)
                    if h < hops[way]:
                        send(kbundle(g, zz), kbundle(g, zz), WAZ[way] + 2 * h + g, zdev(-steps[way]))

    v_hop(1)
    local[0].wait()
    for o in range(1, 4):
        arrive(kpiece(lax.rem(y + 4 - o, 4), z), WAY + o - 1)
    k_hop(0)
    v_hop(2)
    v_hop(3)
    k_hop(1)
    v_hop(4)
    local[1].wait()
    y_up, y_down, y_far = lax.rem(y + 1, 4), lax.rem(y + 3, 4), lax.rem(y + 2, 4)
    send(vbundle(y, 0, NZ), vbundle(y, 0, NZ), WBY, ydev(1)[1])
    send(vbundle(y, 0, NZ), vbundle(y, 0, NZ), WBY + 1, ydev(3)[1])
    k_hop(2)
    arrive(vbundle(y_down, 0, NZ), WBY)
    send(vbundle(y_down, 0, 4), vbundle(y_down, 0, 4), WBY + 2, ydev(1)[1])
    arrive(vbundle(y_up, 0, NZ), WBY + 1)
    send(vbundle(y_up, 4, 4), vbundle(y_up, 4, 4), WBY + 3, ydev(3)[1])
    k_hop(3)
    k_hop(4)
    arrive(vbundle(y_far, 0, 4), WBY + 2)
    arrive(vbundle(y_far, 4, 4), WBY + 3)

    def project(xc):
        rows = hbuf[pl.ds(2 * xc, 2)].reshape(256, 4096)
        weight = wbuf[...].reshape(4096, 2 * HD)
        result = jnp.dot(rows, weight, preferred_element_type=jnp.float32)
        at = pl.ds(pl.multiple_of(xc * 256, 256), 256)
        key = result[:, :HD]
        key = key * cos_ref[at, :] + pltpu.roll(key, HD // 2, 1) * sin_ref[at, :]
        kvbuf[0, pl.ds(2 * xc, 2), 0] = key.astype(jnp.bfloat16).reshape(2, 128, HD)
        kvbuf[0, pl.ds(2 * xc, 2), 1] = result[:, HD:].astype(jnp.bfloat16).reshape(2, 128, HD)

    chunk = (x, x + 1 - 2 * lax.rem(x, 2), 3 - x, lax.rem(x + 2, 4))

    def kv_region(d, c):
        return kvbuf.at[d, pl.ds(2 * chunk[c], 2)]

    def pass_on(d, c):
        if d > 1:
            arrive(kv_region(d - 1, c), KV + (d - 2) * 4 + c)
        send(kv_region(d - 1, c), kv_region(d, c), KV + (d - 1) * 4 + c, next_blk)

    local[2].wait()
    arrive(hbuf.at[partner], HP)
    project(chunk[0])
    pass_on(1, 0)

    def half_rows(slot, half):
        return hbuf.at[slot, pl.ds(half * 64, 64)]

    for half in range(2):
        arrive(half_rows(u_minus, half), HX + half)
        if half == 0:
            send(half_rows(u_minus, 0), half_rows(u_minus, 0), HR, ul(u_plus))
        send(half_rows(u_minus, half), half_rows(u_minus, half), HP + 1 + half, ul(partner))
        arrive(half_rows(u_plus, half), HX + 2 + half)
        if half == 1:
            send(half_rows(u_plus, 1), half_rows(u_plus, 1), HR + 1, ul(u_minus))
        send(half_rows(u_plus, half), half_rows(u_plus, half), HP + 3 + half, ul(partner))
        pass_on(2 + half, 0)

    p_minus, p_plus, p_far = (lax.rem(partner + UL - 2, UL), lax.rem(partner + 2, UL), lax.rem(partner + 4, UL))
    for half in range(2):
        arrive(half_rows(p_minus, half), HP + 1 + half)
        arrive(half_rows(p_plus, half), HP + 3 + half)
    project(chunk[1])
    pass_on(1, 1)
    project(chunk[2])
    pass_on(1, 2)

    m_ref[...] = jnp.full_like(m_ref, NEG)
    l_ref[...] = jnp.zeros_like(l_ref)
    acc_ref[...] = jnp.zeros_like(acc_ref)
    local[3].wait()
    for o in range(1, UL):
        arrive(qbuf.at[lax.rem(u + UL - o, UL)], QX + o - 1)

    def rope_slice(s, carry):
        at = pl.ds(pl.multiple_of(s * 128, 128), 128)
        cosine = cos_ref[at, :]
        sine = sin_ref[at, :]
        for head in range(2):
            q = qbuf[s, :, head * HD : (head + 1) * HD].astype(jnp.float32)
            q = q * cosine + pltpu.roll(q, HD // 2, 1) * sine
            place = (s // 4) * 4 + head * 2 + lax.rem(s, 4) // 2
            qrot[place, pl.ds(pl.multiple_of(lax.rem(s, 2) * 128, 128), 128)] = q.astype(jnp.bfloat16)
        return carry

    lax.fori_loop(0, UL, rope_slice, 0)

    def attend(qh, d, kh):
        source = lax.rem(blk + 16 - d, 16)
        key_order = order_ref[0, 2 * source + kh]
        query_order = order_ref[0, 2 * blk + qh]
        shut = key_order > query_order
        low = jnp.where(shut, -FAR, 0.0)
        lift = jnp.where(shut, FAR, 0.0)

        def rows_of(i, carry):
            place = qh * 4 + i
            keys = kvbuf[d, pl.ds(4 * kh, 4), 0].reshape(512, HD)
            values = kvbuf[d, pl.ds(4 * kh, 4), 1].reshape(512, HD)
            score = lax.dot_general(
                qrot[place], keys, (((1,), (1,)), ((), ())), preferred_element_type=jnp.float32
            )
            if d == 0:
                first = lax.rem(i, 2) * 256 + 1024 * lax.rem(qh + kh, 2)
                row = lax.broadcasted_iota(jnp.int32, score.shape, 0) + first
                column = lax.broadcasted_iota(jnp.int32, score.shape, 1)
                score = jnp.where(row >= column, score, NEG)
            old = m_ref[place]
            top = jnp.max(score, axis=1, keepdims=True) + low
            new = jnp.maximum(old, top)
            base = new + lift
            weight = jnp.exp2((score - jnp.tile(base, (1, 4))) * SCALE2)
            shrink = jnp.exp2((old - new) * SCALE2)
            part = (weight[:, :128] + weight[:, 128:256]) + (weight[:, 256:384] + weight[:, 384:])
            l_ref[place] = l_ref[place] * shrink + part
            acc_ref[place] = acc_ref[place] * shrink + jnp.dot(
                weight.astype(jnp.bfloat16), values, preferred_element_type=jnp.float32
            )
            m_ref[place] = new
            return carry

        lax.fori_loop(0, 4, rows_of, 0)

    own = x // 2
    oth = 1 - own

    attend(0, 0, own)
    pass_on(2, 1)
    attend(1, 0, own)
    pass_on(2, 2)
    attend(0, 1, own)
    pass_on(3, 1)
    attend(1, 1, own)
    pass_on(3, 2)
    arrive(half_rows(u_far, 0), HR)
    send(half_rows(u_far, 0), half_rows(u_far, 0), HP + 5, ul(partner))
    arrive(half_rows(u_far, 1), HR + 1)
    send(half_rows(u_far, 1), half_rows(u_far, 1), HP + 6, ul(partner))
    attend(0, 2, own)
    for half in range(2):
        arrive(half_rows(p_far, half), HP + 5 + half)
    project(chunk[3])
    pass_on(1, 3)
    attend(1, 2, own)
    attend(0, 0, oth)
    pass_on(2, 3)
    attend(1, 0, oth)
    arrive(kv_region(3, 0), KV + 8)
    arrive(kv_region(3, 1), KV + 9)
    attend(0, 3, own)
    pass_on(3, 3)
    attend(1, 3, own)
    for qh in range(2):
        attend(qh, 1, oth)
    for qh in range(2):
        attend(qh, 2, oth)
    arrive(kv_region(3, 2), KV + 10)
    arrive(kv_region(3, 3), KV + 11)
    for qh in range(2):
        attend(qh, 3, oth)

    for qh in range(2):
        for head in range(2):
            for sub in range(2):
                place = qh * 4 + head * 2 + sub
                total = jnp.sum(l_ref[place], axis=1, keepdims=True)
                value = (acc_ref[place] / total).astype(jnp.bfloat16)
                obuf[qh * 4 + sub * 2 : qh * 4 + sub * 2 + 2, :, head * HD : (head + 1) * HD] = value.reshape(2, 128, HD)
    own_out = pltpu.make_async_copy(
        obuf.at[u], out.at[:, pl.ds(pl.multiple_of(u * 2 * HD, HD), 2 * HD)], lsem.at[4]
    )
    own_out.start()
    here = out.at[:, pl.ds(pl.multiple_of(u * 2 * HD, HD), 2 * HD)]
    for o in range(1, UL):
        peer = lax.rem(u + o, UL)
        send(obuf.at[peer], here, OX + o - 1, ul(peer))
    own_out.wait()
    for o in range(1, UL):
        source = lax.rem(u + UL - o, UL)
        arrive(out.at[:, pl.ds(pl.multiple_of(source * 2 * HD, HD), 2 * HD)], OX + o - 1)
    for copy in sends:
        copy.wait_send()


def shards(hidden_in, queries, pair_weight, span_order, yarn_divisor):
    blk = lax.axis_index("blk")
    order_row = span_order[0]
    spans = lax.dynamic_slice(order_row, (2 * blk,), (2,))
    pos = (spans[:, None] * 512 + jnp.arange(512, dtype=jnp.int32)[None, :]).reshape(1024)
    scaled = 2.0 * jnp.arange(HD // 2, dtype=jnp.float32) / HD
    inverse = jnp.exp(-LOG_BASE * scaled) / yarn_divisor.astype(jnp.float32)
    angle = pos.astype(jnp.float32)[:, None] * inverse[None, :]
    cosine = jnp.cos(angle)
    sine = jnp.sin(angle)
    cosine = jnp.concatenate([cosine, cosine], axis=1)
    sine = jnp.concatenate([-sine, sine], axis=1)
    anywhere = pl.BlockSpec(memory_space=pl.ANY)
    vmem = pl.BlockSpec(memory_space=pltpu.VMEM)
    out = pl.pallas_call(
        kernel,
        out_shape=jax.ShapeDtypeStruct((128, QH * HD), jnp.bfloat16),
        in_specs=[pl.BlockSpec(memory_space=pltpu.SMEM), anywhere, anywhere, anywhere, vmem, vmem],
        out_specs=anywhere,
        scratch_shapes=[
            pltpu.VMEM((2, 2, NZ, 128, 2 * HD), jnp.bfloat16),
            pltpu.VMEM((UL, 128, 4096), jnp.bfloat16),
            pltpu.VMEM((UL, 128, 2 * HD), jnp.bfloat16),
            pltpu.VMEM((8, 256, HD), jnp.bfloat16),
            pltpu.VMEM((STEPS + 1, UL, 2, 128, HD), jnp.bfloat16),
            pltpu.VMEM((8, 256, HD), jnp.float32),
            pltpu.VMEM((8, 256, HD), jnp.float32),
            pltpu.VMEM((8, 256, HD), jnp.float32),
            pltpu.VMEM((UL, 128, 2 * HD), jnp.bfloat16),
            pltpu.SemaphoreType.DMA((80,)),
            pltpu.SemaphoreType.DMA((80,)),
            pltpu.SemaphoreType.DMA((5,)),
        ],
        compiler_params=pltpu.CompilerParams(
            collective_id=0, has_side_effects=True, vmem_limit_bytes=48 * 1024 * 1024
        ),
    )(span_order, hidden_in[0], queries[0], pair_weight, cosine, sine)
    return out[None]


def solution(mesh):
    return jax.shard_map(
        shards,
        mesh=mesh,
        in_specs=(
            P("dp", ("blk", "ulysses"), None),
            P("dp", ("blk", "ulysses"), None),
            P(("dp", "blk"), None),
            P("dp", None),
            P(),
        ),
        out_specs=P("dp", ("blk", "ulysses"), None),
        check_vma=False,
    )
```

```python
import math

import jax
import jax.numpy as jnp
from jax import lax
from jax.experimental import pallas as pl
from jax.experimental.pallas import tpu as pltpu
from jax.sharding import PartitionSpec as P
import numpy as np

KVH = 8
HD = 128
QH = 16
STEPS = 3
UL = 8
NZ = 8
LOG_BASE = math.log(500000.0)
MESH = pl.DeviceIdType.MESH
SCALE2 = (1.0 / math.sqrt(HD)) * math.log2(math.e)
NEG = -1.0e30
FREQUENCIES = [
    float(np.exp(np.float32(-LOG_BASE) * (np.float32(2 * f) / np.float32(HD)), dtype=np.float32)) for f in range(HD // 2)
]
FAR = 2.0e30


def wrap(value, size):
    return lax.rem(value + size, size)


def kernel(
    order_hbm, divisor_hbm, hid, qry, pw, out,
    order_ref, divisor_ref, cos_ref, sin_ref, wbuf, hbuf, qbuf, qrot, kvbuf, m_ref, l_ref, acc_ref, obuf,
    ssem, rsem, lsem,
):
    dp = lax.axis_index("dp")
    u = lax.axis_index("ulysses")
    blk = lax.axis_index("blk")
    core = lax.rem(u, 2)
    other_core = 1 - core
    x = u // 2
    yh = blk // NZ
    z = lax.rem(blk, NZ)
    y = yh * 2 + dp

    counter = [0]

    def take(n):
        base = counter[0]
        counter[0] += n
        return base

    def ul(index):
        return {"ulysses": index}

    def chip(offset, on_core):
        return ul(2 * lax.rem(x + offset, 4) + on_core)

    def ydev(offset):
        other = lax.rem(y + offset, 4)
        return {"dp": lax.rem(other, 2), "blk": (other // 2) * NZ + z}

    def zdev(offset):
        return {"blk": yh * NZ + wrap(z + offset, NZ)}

    x_plus, x_far, x_minus = lax.rem(x + 1, 4), lax.rem(x + 2, 4), lax.rem(x + 3, 4)
    partner = u + 1 - 2 * core
    next_blk = {"blk": lax.rem(blk + 1, 16)}
    prev_blk = {"blk": lax.rem(blk + 15, 16)}

    def rcopy(src, dst, index, device):
        return pltpu.make_async_remote_copy(
            src_ref=src, dst_ref=dst, send_sem=ssem.at[index], recv_sem=rsem.at[index],
            device_id=device, device_id_type=MESH,
        )

    sends = []

    def send(src, dst, index, device):
        copy = rcopy(src, dst, index, device)
        copy.start()
        sends.append(copy)

    def arrive(dst, index):
        rcopy(dst, dst, index, ul(partner)).wait_recv()

    own_k = pw.at[:, pl.ds(pl.multiple_of(u * HD, HD), HD)]
    own_v = pw.at[:, pl.ds(pl.multiple_of(KVH * HD + u * HD, HD), HD)]
    WB = (take(4), take(3))
    WAY = take(3)
    WAZ = (take(8), take(8))
    WBY = (take(8), take(8))
    WBF = take(8)
    HX, HR, HP = take(4), take(2), take(8)
    QX = take(7)
    KV = take(24)
    OX = take(7)

    def vpiece(yy, zz):
        return wbuf.at[lax.rem(yy, 2), yy // 2, zz, :, pl.ds(HD, HD)]

    def kpiece(yy, zz):
        return wbuf.at[lax.rem(yy, 2), yy // 2, zz, :, pl.ds(0, HD)]

    def kbundle(g, zz):
        return wbuf.at[g, :, zz, :, pl.ds(0, HD)]

    def hid_half(a):
        return hid.at[pl.ds(a * 64, 64)]

    def qry_for(index):
        return qry.at[:, pl.ds(pl.multiple_of(index * 2 * HD, HD), 2 * HD)]

    local = [
        pltpu.make_async_copy(own_k, kpiece(y, z), lsem.at[0]),
        pltpu.make_async_copy(own_v, vpiece(y, z), lsem.at[1]),
        pltpu.make_async_copy(hid_half(0), hbuf.at[x, 0, core], lsem.at[2]),
        pltpu.make_async_copy(hid_half(1), hbuf.at[x, 1, core], lsem.at[3]),
        pltpu.make_async_copy(qry_for(u), qbuf.at[u], lsem.at[4]),
        pltpu.make_async_copy(order_hbm, order_ref, lsem.at[6]),
        pltpu.make_async_copy(divisor_hbm, divisor_ref, lsem.at[7]),
    ]
    for copy in local:
        copy.start()

    barrier = pltpu.get_barrier_semaphore()
    greet = [ul(lax.rem(u + o, UL)) for o in range(1, UL)]
    greet += [ydev(o) for o in range(1, 4)]
    greet += [zdev(1), zdev(-1), next_blk, prev_blk]
    for device in greet:
        pl.semaphore_signal(barrier, inc=1, device_id=device, device_id_type=MESH)
    pl.semaphore_wait(barrier, len(greet))

    send(own_v, vpiece(y, z), WB[0], zdev(1))
    send(own_v, vpiece(y, z), WB[1], zdev(-1))
    for o in (2, 1, 3):
        send(own_k, kpiece(y, z), WAY + o - 1, ydev(o))
    for a in range(2):
        send(hid_half(a), hbuf.at[x, a, core], HX + a, chip(1, core))
        send(hid_half(a), hbuf.at[x, a, core], HX + 2 + a, chip(3, core))
        send(hid_half(a), hbuf.at[x, a, core], HP + a, ul(partner))
        if a == 0:
            for o in range(1, UL):
                peer = lax.rem(u + o, UL)
                send(qry_for(peer), qbuf.at[u], QX + o - 1, ul(peer))

    spots = {0: 0, -1: 1, 1: 2, -2: 3, 2: 4, -3: 5, 3: 6, -4: 7}
    y_up, y_down, y_far = lax.rem(y + 1, 4), lax.rem(y + 3, 4), lax.rem(y + 2, 4)

    def v_spread(offset, source=None):
        zz = wrap(z + offset, NZ)
        src = vpiece(y, zz) if source is None else source
        send(src, vpiece(y, zz), WBY[0] + spots[offset], ydev(1))
        send(src, vpiece(y, zz), WBY[1] + spots[offset], ydev(3))

    def v_hop(h):
        for way, step in ((0, -1), (1, 1)):
            if h <= (4, 3)[way]:
                zz = wrap(z + step * h, NZ)
                arrive(vpiece(y, zz), WB[way] + h - 1)
                if h < (4, 3)[way]:
                    send(vpiece(y, zz), vpiece(y, zz), WB[way] + h, zdev(-step))
                v_spread(step * h)

    def v_across(*offsets):
        for offset in offsets:
            zz = wrap(z + offset, NZ)
            spot = spots[offset]
            arrive(vpiece(y_down, zz), WBY[0] + spot)
            if spot % 2 == 0:
                send(vpiece(y_down, zz), vpiece(y_down, zz), WBF + spot, ydev(1))
            arrive(vpiece(y_up, zz), WBY[1] + spot)
            if spot % 2 == 1:
                send(vpiece(y_up, zz), vpiece(y_up, zz), WBF + spot, ydev(3))

    def k_hop(h):
        for g in range(2):
            for way, step in ((0, -1), (1, 1)):
                last = 4 if g == way else 3
                if h <= last:
                    zz = wrap(z + step * h, NZ)
                    if h > 0:
                        arrive(kbundle(g, zz), WAZ[way] + 2 * (h - 1) + g)
                    if h < last:
                        send(kbundle(g, zz), kbundle(g, zz), WAZ[way] + 2 * h + g, zdev(-step))

    v_spread(0, own_v)
    v_hop(1)
    local[0].wait()
    for o in range(1, 4):
        arrive(kpiece(lax.rem(y + 4 - o, 4), z), WAY + o - 1)
    k_hop(0)
    v_hop(2)
    v_across(0)
    v_hop(3)
    v_across(-1, 1)
    k_hop(1)
    v_hop(4)
    v_across(-2, 2)
    k_hop(2)

    local[5].wait()
    local[6].wait()
    lane64 = lax.broadcasted_iota(jnp.int32, (1, HD // 2), 1)
    inverse = jnp.zeros((1, HD // 2), jnp.float32)
    for f, value in enumerate(FREQUENCIES):
        inverse = jnp.where(lane64 == f, value, inverse)
    inverse = inverse / divisor_ref[...].astype(jnp.float32)
    inverse = jnp.concatenate([inverse, inverse], axis=1)

    def table(i, carry):
        start = order_ref[0, 2 * blk + i // 4] * 512 + lax.rem(i, 4) * 128
        pos = lax.broadcasted_iota(jnp.int32, (128, HD), 0) + start
        angle = pos.astype(jnp.float32) * inverse
        lane = lax.broadcasted_iota(jnp.int32, (128, HD), 1)
        sine = jnp.sin(angle)
        at = pl.ds(pl.multiple_of(i * 128, 128), 128)
        cos_ref[at, :] = jnp.cos(angle)
        sin_ref[at, :] = jnp.where(lane < HD // 2, -sine, sine)
        return carry

    lax.fori_loop(0, UL, table, 0)
    m_ref[...] = jnp.full_like(m_ref, NEG)
    l_ref[...] = jnp.zeros_like(l_ref)
    acc_ref[...] = jnp.zeros_like(acc_ref)

    v_across(-3, 3)
    k_hop(3)
    v_across(-4)
    k_hop(4)
    for offset in spots:
        arrive(vpiece(y_far, wrap(z + offset, NZ)), WBF + spots[offset])
    local[1].wait()

    chunk = (x, x + 1 - 2 * lax.rem(x, 2), 3 - x, x_far)
    pieces = ((0, 0), (0, 1), (1, 0), (2, 0), (1, 1), (2, 1), (3, 0), (3, 1))

    def project(n):
        xc, a = chunk[pieces[n][0]], pieces[n][1]
        rows = hbuf[xc, a].reshape(128, 4096)
        weight = wbuf[...].reshape(4096, 2 * HD)
        result = jnp.dot(rows, weight, preferred_element_type=jnp.float32)
        key = result[:, :HD]
        turned = pltpu.roll(key, HD // 2, 1)
        for k in range(2):
            at = pl.ds(pl.multiple_of(xc * 256 + k * 128 + a * 64, 64), 64)
            part = slice(k * 64, (k + 1) * 64)
            rope = key[part] * cos_ref[at, :] + turned[part] * sin_ref[at, :]
            kvbuf[0, xc, a, 0, part] = rope.astype(jnp.bfloat16)
        kvbuf[0, xc, a, 1] = result[:, HD:].T.astype(jnp.bfloat16)
        pass_on(1, n)

    def kv_region(d, n):
        return kvbuf.at[d, chunk[pieces[n][0]], pieces[n][1]]

    def landed(d, n):
        arrive(kv_region(d, n), KV + (d - 1) * 8 + n)

    def pass_on(d, n):
        if d > 1:
            landed(d - 1, n)
        send(kv_region(d - 1, n), kv_region(d, n), KV + (d - 1) * 8 + n, next_blk)

    def side(a):
        arrive(hbuf.at[x_minus, a, core], HX + a)
        if a == 1:
            send(hbuf.at[x_minus, 1, core], hbuf.at[x_minus, 1, core], HR + 1, chip(1, core))
        send(hbuf.at[x_minus, a, core], hbuf.at[x_minus, a, core], HP + 2 + a, ul(partner))
        arrive(hbuf.at[x_plus, a, core], HX + 2 + a)
        if a == 0:
            send(hbuf.at[x_plus, 0, core], hbuf.at[x_plus, 0, core], HR, chip(3, core))
        send(hbuf.at[x_plus, a, core], hbuf.at[x_plus, a, core], HP + 4 + a, ul(partner))

    def side_partner(a):
        arrive(hbuf.at[x_minus, a, other_core], HP + 2 + a)
        arrive(hbuf.at[x_plus, a, other_core], HP + 4 + a)

    for a in range(2):
        local[2 + a].wait()
        arrive(hbuf.at[x, a, other_core], HP + a)
        project(a)
    side(0)
    side_partner(0)
    project(2)
    project(3)

    local[4].wait()
    for o in range(1, UL):
        arrive(qbuf.at[lax.rem(u + UL - o, UL)], QX + o - 1)

    def rope_slice(s, carry):
        at = pl.ds(pl.multiple_of(s * 128, 128), 128)
        cosine = cos_ref[at, :]
        sine = sin_ref[at, :]
        for head in range(2):
            q = qbuf[s, :, head * HD : (head + 1) * HD].astype(jnp.float32)
            q = q * cosine + pltpu.roll(q, HD // 2, 1) * sine
            place = (s // 2) * 2 + head
            qrot[place, pl.ds(pl.multiple_of(lax.rem(s, 2) * 128, 128), 128)] = q.astype(jnp.bfloat16)
        return carry

    lax.fori_loop(0, UL, rope_slice, 0)

    def attend(first, count, *tiles):
        def one_chip(i, carry):
            j = first + i
            query_order = order_ref[0, 2 * blk + j // 2]
            lows, lifts = [], []
            for d, c in tiles:
                source = lax.rem(blk + 16 - d, 16)
                shut = order_ref[0, 2 * source + chunk[c] // 2] > query_order
                lows.append(jnp.where(shut, -FAR, 0.0))
                lifts.append(jnp.where(shut, FAR, 0.0))
            for head in range(2):
                place = 2 * j + head
                query = qrot[place]
                old = m_ref[place]
                new = old
                scores = []
                for (d, c), low in zip(tiles, lows):
                    keys = kvbuf[d, chunk[c], :, 0].reshape(256, HD)
                    score = lax.dot_general(
                        keys, query, (((1,), (1,)), ((), ())), preferred_element_type=jnp.float32
                    )
                    if d == 0:
                        row = lax.broadcasted_iota(jnp.int32, score.shape, 0)
                        shift = (lax.shift_right_logical(row, 6) & 1) - lax.shift_right_logical(row, 7)
                        key_at = row + 64 * shift + lax.rem(chunk[c], 2) * 256
                        apart = lax.rem(chunk[c] // 2 + j // 2, 2)
                        query_at = lax.broadcasted_iota(jnp.int32, score.shape, 1) + (
                            lax.rem(j, 2) * 256 + apart * 1024
                        )
                        score = jnp.where(query_at >= key_at, score, 4.0 * NEG)
                    scores.append(score)
                    new = jnp.maximum(new, jnp.max(score, axis=0, keepdims=True) + low)
                shrink = jnp.exp2((old - new) * SCALE2)
                total = l_ref[place] * shrink
                mixed = acc_ref[place] * shrink
                for (d, c), score, lift in zip(tiles, scores, lifts):
                    weight = jnp.exp2((score - (new + lift)) * SCALE2)
                    total = total + jnp.sum(weight.reshape(32, 8, 256), axis=0)
                    values = jnp.concatenate([kvbuf[d, chunk[c], 0, 1], kvbuf[d, chunk[c], 1, 1]], axis=1)
                    mixed = mixed + jnp.dot(
                        values, weight.astype(jnp.bfloat16), preferred_element_type=jnp.float32
                    )
                l_ref[place] = total
                acc_ref[place] = mixed
                m_ref[place] = new
            return carry

        lax.fori_loop(0, count, one_chip, 0)

    pass_on(2, 0)
    pass_on(2, 1)
    pass_on(2, 2)
    pass_on(2, 3)
    attend(0, 2, (0, 0), (1, 0))
    pass_on(3, 0)
    pass_on(3, 1)
    attend(2, 2, (0, 0), (1, 0))
    side(1)
    side_partner(1)
    project(4)
    project(5)
    pass_on(3, 2)
    pass_on(3, 3)
    attend(0, 4, (0, 1), (0, 2))
    pass_on(2, 4)
    pass_on(2, 5)
    landed(3, 0)
    landed(3, 1)
    attend(0, 2, (2, 0), (3, 0))
    pass_on(3, 4)
    pass_on(3, 5)
    attend(2, 2, (2, 0), (3, 0))
    arrive(hbuf.at[x_far, 0, core], HR)
    send(hbuf.at[x_far, 0, core], hbuf.at[x_far, 0, core], HP + 6, ul(partner))
    attend(0, 2, (1, 1), (1, 2))
    arrive(hbuf.at[x_far, 0, other_core], HP + 6)
    project(6)
    arrive(hbuf.at[x_far, 1, core], HR + 1)
    send(hbuf.at[x_far, 1, core], hbuf.at[x_far, 1, core], HP + 7, ul(partner))
    attend(2, 2, (1, 1), (1, 2))
    arrive(hbuf.at[x_far, 1, other_core], HP + 7)
    project(7)
    pass_on(2, 6)
    attend(0, 2, (2, 1), (2, 2))
    pass_on(2, 7)
    attend(2, 2, (2, 1), (2, 2))
    pass_on(3, 6)
    for n in (2, 4):
        landed(3, n)
    attend(0, 2, (0, 3), (3, 1))
    pass_on(3, 7)
    attend(2, 2, (0, 3), (3, 1))
    for n in (3, 5):
        landed(3, n)
    attend(0, 4, (3, 2), (1, 3))
    attend(0, 4, (2, 3))
    for n in (6, 7):
        landed(3, n)

    here = out.at[:, pl.ds(pl.multiple_of(u * 2 * HD, HD), 2 * HD)]
    own_out = pltpu.make_async_copy(obuf.at[u], here, lsem.at[5])
    for offset in (2, 1, 3, 0):
        j = lax.rem(x + offset, 4)
        attend(j, 1, (3, 3))
        for head in range(2):
            place = 2 * j + head
            total = jnp.sum(l_ref[place], axis=0, keepdims=True)
            value = (acc_ref[place] / total).T.astype(jnp.bfloat16)
            obuf[pl.ds(2 * j, 2), :, head * HD : (head + 1) * HD] = value.reshape(2, 128, HD)
        if offset:
            for k, to in enumerate((core, other_core)):
                send(obuf.at[2 * j + to], here, OX + (offset - 1) * 2 + k, ul(2 * j + to))
        else:
            own_out.start()
            send(obuf.at[partner], here, OX + 6, ul(partner))
    own_out.wait()

    def out_from(index):
        return out.at[:, pl.ds(pl.multiple_of(index * 2 * HD, HD), 2 * HD)]

    for offset in (2, 1, 3):
        for k, source_core in enumerate((core, other_core)):
            arrive(out_from(2 * lax.rem(x + 4 - offset, 4) + source_core), OX + (offset - 1) * 2 + k)
    arrive(out_from(partner), OX + 6)
    for copy in sends:
        copy.wait_send()


def shards(hidden_in, queries, pair_weight, span_order, yarn_divisor):
    anywhere = pl.BlockSpec(memory_space=pl.ANY)
    hbm = pl.BlockSpec(memory_space=pltpu.HBM)
    out = pl.pallas_call(
        kernel,
        out_shape=jax.ShapeDtypeStruct((128, QH * HD), jnp.bfloat16),
        in_specs=[
            hbm, hbm, hbm, hbm, hbm,
        ],
        out_specs=anywhere,
        scratch_shapes=[
            pltpu.SMEM((1, 32), jnp.int32),
            pltpu.VMEM((1, HD // 2), jnp.int32),
            pltpu.VMEM((1024, HD), jnp.float32),
            pltpu.VMEM((1024, HD), jnp.float32),
            pltpu.VMEM((2, 2, NZ, 128, 2 * HD), jnp.bfloat16),
            pltpu.VMEM((4, 2, 2, 64, 4096), jnp.bfloat16),
            pltpu.VMEM((UL, 128, 2 * HD), jnp.bfloat16),
            pltpu.VMEM((8, 256, HD), jnp.bfloat16),
            pltpu.VMEM((STEPS + 1, 4, 2, 2, 128, HD), jnp.bfloat16),
            pltpu.VMEM((8, 1, 256), jnp.float32),
            pltpu.VMEM((8, 8, 256), jnp.float32),
            pltpu.VMEM((8, HD, 256), jnp.float32),
            pltpu.VMEM((UL, 128, 2 * HD), jnp.bfloat16),
            pltpu.SemaphoreType.DMA((104,)),
            pltpu.SemaphoreType.DMA((104,)),
            pltpu.SemaphoreType.DMA((8,)),
        ],
        compiler_params=pltpu.CompilerParams(
            collective_id=0, has_side_effects=True, vmem_limit_bytes=61900 * 1024
        ),
    )(span_order, yarn_divisor[None, :], hidden_in[0], queries[0], pair_weight)
    return out[None]


def solution(mesh):
    return jax.shard_map(
        shards,
        mesh=mesh,
        in_specs=(
            P("dp", ("blk", "ulysses"), None),
            P("dp", ("blk", "ulysses"), None),
            P(("dp", "blk"), None),
            P("dp", None),
            P(),
        ),
        out_specs=P("dp", ("blk", "ulysses"), None),
        check_vma=False,
    )
```

```python
import math

import jax
import jax.numpy as jnp
from jax import lax
from jax.experimental import pallas as pl
from jax.experimental.pallas import tpu as pltpu
from jax.sharding import PartitionSpec as P
import numpy as np

KVH = 8
HD = 128
QH = 16
STEPS = 3
UL = 8
NZ = 8
LOG_BASE = math.log(500000.0)
MESH = pl.DeviceIdType.MESH
SCALE2 = (1.0 / math.sqrt(HD)) * math.log2(math.e)
NEG = -1.0e30
FREQUENCIES = [
    float(np.exp(np.float32(-LOG_BASE) * (np.float32(2 * f) / np.float32(HD)), dtype=np.float32)) for f in range(HD // 2)
]
FAR = 2.0e30


def wrap(value, size):
    return lax.rem(value + size, size)


def kernel(
    order_hbm, divisor_hbm, hid, qry, pw, out,
    order_ref, divisor_ref, cos_ref, sin_ref, wbuf, hbuf, qbuf, qrot, kvbuf, m_ref, l_ref, acc_ref, obuf,
    sa_ref, sb_ref, ta_ref, tb_ref, ssem, rsem, lsem,
):
    dp = lax.axis_index("dp")
    u = lax.axis_index("ulysses")
    blk = lax.axis_index("blk")
    core = lax.rem(u, 2)
    other_core = 1 - core
    x = u // 2
    yh = blk // NZ
    z = lax.rem(blk, NZ)
    y = yh * 2 + dp

    counter = [0]

    def take(n):
        base = counter[0]
        counter[0] += n
        return base

    def ul(index):
        return {"ulysses": index}

    def chip(offset, on_core):
        return ul(2 * lax.rem(x + offset, 4) + on_core)

    def ydev(offset):
        other = lax.rem(y + offset, 4)
        return {"dp": lax.rem(other, 2), "blk": (other // 2) * NZ + z}

    def zdev(offset):
        return {"blk": yh * NZ + wrap(z + offset, NZ)}

    x_plus, x_far, x_minus = lax.rem(x + 1, 4), lax.rem(x + 2, 4), lax.rem(x + 3, 4)
    partner = u + 1 - 2 * core
    next_blk = {"blk": lax.rem(blk + 1, 16)}
    prev_blk = {"blk": lax.rem(blk + 15, 16)}

    def rcopy(src, dst, index, device):
        return pltpu.make_async_remote_copy(
            src_ref=src, dst_ref=dst, send_sem=ssem.at[index], recv_sem=rsem.at[index],
            device_id=device, device_id_type=MESH,
        )

    sends = []

    def send(src, dst, index, device):
        copy = rcopy(src, dst, index, device)
        copy.start()
        sends.append(copy)

    def arrive(dst, index):
        rcopy(dst, dst, index, ul(partner)).wait_recv()

    own_k = pw.at[:, pl.ds(pl.multiple_of(u * HD, HD), HD)]
    own_v = pw.at[:, pl.ds(pl.multiple_of(KVH * HD + u * HD, HD), HD)]
    WB = (take(4), take(3))
    WAY = take(3)
    WAZ = (take(8), take(8))
    WBY = (take(8), take(8))
    WBF = take(8)
    HX, HR, HP = take(4), take(2), take(8)
    QX = take(7)
    KV = take(24)
    OX = take(7)

    def vpiece(yy, zz):
        return wbuf.at[lax.rem(yy, 2), yy // 2, zz, :, pl.ds(HD, HD)]

    def kpiece(yy, zz):
        return wbuf.at[lax.rem(yy, 2), yy // 2, zz, :, pl.ds(0, HD)]

    def kbundle(g, zz):
        return wbuf.at[g, :, zz, :, pl.ds(0, HD)]

    def hid_half(a):
        return hid.at[pl.ds(a * 64, 64)]

    def qry_for(index):
        return qry.at[:, pl.ds(pl.multiple_of(index * 2 * HD, HD), 2 * HD)]

    local = [
        pltpu.make_async_copy(own_k, kpiece(y, z), lsem.at[0]),
        pltpu.make_async_copy(own_v, vpiece(y, z), lsem.at[1]),
        pltpu.make_async_copy(hid_half(0), hbuf.at[x, 0, core], lsem.at[2]),
        pltpu.make_async_copy(hid_half(1), hbuf.at[x, 1, core], lsem.at[3]),
        pltpu.make_async_copy(qry_for(u), qbuf.at[u], lsem.at[4]),
        pltpu.make_async_copy(order_hbm, order_ref, lsem.at[6]),
        pltpu.make_async_copy(divisor_hbm, divisor_ref, lsem.at[7]),
    ]
    for copy in local:
        copy.start()

    barrier = pltpu.get_barrier_semaphore()
    greet = [ul(lax.rem(u + o, UL)) for o in range(1, UL)]
    greet += [ydev(o) for o in range(1, 4)]
    greet += [zdev(1), zdev(-1), next_blk, prev_blk]
    for device in greet:
        pl.semaphore_signal(barrier, inc=1, device_id=device, device_id_type=MESH)
    pl.semaphore_wait(barrier, len(greet))

    send(own_v, vpiece(y, z), WB[0], zdev(1))
    send(own_v, vpiece(y, z), WB[1], zdev(-1))
    for o in (2, 1, 3):
        send(own_k, kpiece(y, z), WAY + o - 1, ydev(o))
    for a in range(2):
        send(hid_half(a), hbuf.at[x, a, core], HX + a, chip(1, core))
        send(hid_half(a), hbuf.at[x, a, core], HX + 2 + a, chip(3, core))
        send(hid_half(a), hbuf.at[x, a, core], HP + a, ul(partner))
        if a == 0:
            for o in range(1, UL):
                peer = lax.rem(u + o, UL)
                send(qry_for(peer), qbuf.at[u], QX + o - 1, ul(peer))

    spots = {0: 0, -1: 1, 1: 2, -2: 3, 2: 4, -3: 5, 3: 6, -4: 7}
    y_up, y_down, y_far = lax.rem(y + 1, 4), lax.rem(y + 3, 4), lax.rem(y + 2, 4)

    def v_spread(offset, source=None):
        zz = wrap(z + offset, NZ)
        src = vpiece(y, zz) if source is None else source
        send(src, vpiece(y, zz), WBY[0] + spots[offset], ydev(1))
        send(src, vpiece(y, zz), WBY[1] + spots[offset], ydev(3))

    def v_hop(h):
        for way, step in ((0, -1), (1, 1)):
            if h <= (4, 3)[way]:
                zz = wrap(z + step * h, NZ)
                arrive(vpiece(y, zz), WB[way] + h - 1)
                if h < (4, 3)[way]:
                    send(vpiece(y, zz), vpiece(y, zz), WB[way] + h, zdev(-step))
                v_spread(step * h)

    def v_across(*offsets):
        for offset in offsets:
            zz = wrap(z + offset, NZ)
            spot = spots[offset]
            arrive(vpiece(y_down, zz), WBY[0] + spot)
            if spot % 2 == 0:
                send(vpiece(y_down, zz), vpiece(y_down, zz), WBF + spot, ydev(1))
            arrive(vpiece(y_up, zz), WBY[1] + spot)
            if spot % 2 == 1:
                send(vpiece(y_up, zz), vpiece(y_up, zz), WBF + spot, ydev(3))

    def k_hop(h):
        for g in range(2):
            for way, step in ((0, -1), (1, 1)):
                last = 4 if g == way else 3
                if h <= last:
                    zz = wrap(z + step * h, NZ)
                    if h > 0:
                        arrive(kbundle(g, zz), WAZ[way] + 2 * (h - 1) + g)
                    if h < last:
                        send(kbundle(g, zz), kbundle(g, zz), WAZ[way] + 2 * h + g, zdev(-step))

    def side(a):
        arrive(hbuf.at[x_minus, a, core], HX + a)
        if a == 1:
            send(hbuf.at[x_minus, 1, core], hbuf.at[x_minus, 1, core], HR + 1, chip(1, core))
        send(hbuf.at[x_minus, a, core], hbuf.at[x_minus, a, core], HP + 2 + a, ul(partner))
        arrive(hbuf.at[x_plus, a, core], HX + 2 + a)
        if a == 0:
            send(hbuf.at[x_plus, 0, core], hbuf.at[x_plus, 0, core], HR, chip(3, core))
        send(hbuf.at[x_plus, a, core], hbuf.at[x_plus, a, core], HP + 4 + a, ul(partner))

    v_spread(0, own_v)
    v_hop(1)
    local[0].wait()
    for o in range(1, 4):
        arrive(kpiece(lax.rem(y + 4 - o, 4), z), WAY + o - 1)
    k_hop(0)
    v_hop(2)
    v_across(0)
    v_hop(3)
    v_across(-1, 1)
    k_hop(1)
    v_hop(4)
    v_across(-2, 2)
    k_hop(2)

    local[5].wait()
    local[6].wait()
    lane64 = lax.broadcasted_iota(jnp.int32, (1, HD // 2), 1)
    inverse = jnp.zeros((1, HD // 2), jnp.float32)
    for f, value in enumerate(FREQUENCIES):
        inverse = jnp.where(lane64 == f, value, inverse)
    inverse = inverse / divisor_ref[...].astype(jnp.float32)
    inverse = jnp.concatenate([inverse, inverse], axis=1)

    def table(i, carry):
        start = order_ref[0, 2 * blk + i // 4] * 512 + lax.rem(i, 4) * 128
        pos = lax.broadcasted_iota(jnp.int32, (128, HD), 0) + start
        angle = pos.astype(jnp.float32) * inverse
        lane = lax.broadcasted_iota(jnp.int32, (128, HD), 1)
        sine = jnp.sin(angle)
        at = pl.ds(pl.multiple_of(i * 128, 128), 128)
        cos_ref[at, :] = jnp.cos(angle)
        sin_ref[at, :] = jnp.where(lane < HD // 2, -sine, sine)
        return carry

    lax.fori_loop(0, UL, table, 0)
    m_ref[...] = jnp.full_like(m_ref, NEG)
    l_ref[...] = jnp.zeros_like(l_ref)
    acc_ref[...] = jnp.zeros_like(acc_ref)

    v_across(-3, 3)
    k_hop(3)
    side(0)
    v_across(-4)
    k_hop(4)
    for offset in spots:
        arrive(vpiece(y_far, wrap(z + offset, NZ)), WBF + spots[offset])
    local[1].wait()

    chunk = (x, x + 1 - 2 * lax.rem(x, 2), 3 - x, x_far)
    pieces = ((0, 0), (0, 1), (1, 0), (2, 0), (1, 1), (2, 1), (3, 0), (3, 1))

    def project(n):
        xc, a = chunk[pieces[n][0]], pieces[n][1]
        rows = hbuf[xc, a].reshape(128, 4096)
        weight = wbuf[...].reshape(4096, 2 * HD)
        result = jnp.dot(rows, weight, preferred_element_type=jnp.float32)
        key = result[:, :HD]
        turned = pltpu.roll(key, HD // 2, 1)
        for k in range(2):
            at = pl.ds(pl.multiple_of(xc * 256 + k * 128 + a * 64, 64), 64)
            part = slice(k * 64, (k + 1) * 64)
            rope = key[part] * cos_ref[at, :] + turned[part] * sin_ref[at, :]
            kvbuf[0, xc, a, 0, part] = rope.astype(jnp.bfloat16)
        kvbuf[0, xc, a, 1] = result[:, HD:].T.astype(jnp.bfloat16)
        pass_on(1, n)

    def kv_region(d, n):
        return kvbuf.at[d, chunk[pieces[n][0]], pieces[n][1]]

    def landed(d, n):
        arrive(kv_region(d, n), KV + (d - 1) * 8 + n)

    def pass_on(d, n):
        if d > 1:
            landed(d - 1, n)
        send(kv_region(d - 1, n), kv_region(d, n), KV + (d - 1) * 8 + n, next_blk)

    def side_partner(a):
        arrive(hbuf.at[x_minus, a, other_core], HP + 2 + a)
        arrive(hbuf.at[x_plus, a, other_core], HP + 4 + a)


    def rope_slice(s, carry):
        at = pl.ds(pl.multiple_of(s * 128, 128), 128)
        cosine = cos_ref[at, :]
        sine = sin_ref[at, :]
        for head in range(2):
            q = qbuf[s, :, head * HD : (head + 1) * HD].astype(jnp.float32)
            q = q * cosine + pltpu.roll(q, HD // 2, 1) * sine
            place = (s // 2) * 2 + head
            qrot[place, pl.ds(pl.multiple_of(lax.rem(s, 2) * 128, 128), 128)] = q.astype(jnp.bfloat16)
        return carry

    def queries():
        local[4].wait()
        for o in range(1, UL):
            arrive(qbuf.at[lax.rem(u + UL - o, UL)], QX + o - 1)
        lax.fori_loop(0, UL, rope_slice, 0)

    def far(a):
        arrive(hbuf.at[x_far, a, core], HR + a)
        send(hbuf.at[x_far, a, core], hbuf.at[x_far, a, core], HP + 6 + a, ul(partner))

    def attend(first, count, *tiles):
        def shut(j, d, c):
            source = lax.rem(blk + 16 - d, 16)
            return order_ref[0, 2 * source + chunk[c] // 2] > order_ref[0, 2 * blk + j // 2]

        def measure(s_ref, top_ref, j, head):
            query = qrot[2 * j + head]
            top = None
            for t, (d, c) in enumerate(tiles):
                keys = kvbuf[d, chunk[c], :, 0].reshape(256, HD)
                score = lax.dot_general(
                    keys, query, (((1,), (1,)), ((), ())), preferred_element_type=jnp.float32
                )
                if d == 0:
                    row = lax.broadcasted_iota(jnp.int32, score.shape, 0)
                    shift = (lax.shift_right_logical(row, 6) & 1) - lax.shift_right_logical(row, 7)
                    key_at = row + 64 * shift + lax.rem(chunk[c], 2) * 256
                    apart = lax.rem(chunk[c] // 2 + j // 2, 2)
                    query_at = lax.broadcasted_iota(jnp.int32, score.shape, 1) + (
                        lax.rem(j, 2) * 256 + apart * 1024
                    )
                    score = jnp.where(query_at >= key_at, score, 4.0 * NEG)
                s_ref[t] = score
                here = jnp.max(score, axis=0, keepdims=True) + jnp.where(shut(j, d, c), -FAR, 0.0)
                top = here if top is None else jnp.maximum(top, here)
            top_ref[...] = top

        def gather(s_ref, top_ref, j, head):
            place = 2 * j + head
            old = m_ref[place]
            new = jnp.maximum(old, top_ref[...])
            shrink = jnp.exp2((old - new) * SCALE2)
            total = l_ref[place] * shrink
            mixed = acc_ref[place] * shrink
            for t, (d, c) in enumerate(tiles):
                base = new + jnp.where(shut(j, d, c), FAR, 0.0)
                weight = jnp.exp2((s_ref[t] - base) * SCALE2)
                total = total + jnp.sum(weight.reshape(32, 8, 256), axis=0)
                values = jnp.concatenate([kvbuf[d, chunk[c], 0, 1], kvbuf[d, chunk[c], 1, 1]], axis=1)
                mixed = mixed + jnp.dot(
                    values, weight.astype(jnp.bfloat16), preferred_element_type=jnp.float32
                )
            l_ref[place] = total
            acc_ref[place] = mixed
            m_ref[place] = new

        measure(sa_ref, ta_ref, first, 0)
        if count == 1:
            measure(sb_ref, tb_ref, first, 1)
            gather(sa_ref, ta_ref, first, 0)
            gather(sb_ref, tb_ref, first, 1)
            return

        def one_chip(i, carry):
            j = first + i
            measure(sb_ref, tb_ref, j, 1)
            gather(sa_ref, ta_ref, j, 0)
            measure(sa_ref, ta_ref, first + jnp.minimum(i + 1, count - 1), 0)
            gather(sb_ref, tb_ref, j, 1)
            return carry

        lax.fori_loop(0, count, one_chip, 0)

    local[2].wait()
    arrive(hbuf.at[x, 0, other_core], HP + 0)
    project(0)
    local[3].wait()
    arrive(hbuf.at[x, 1, other_core], HP + 1)
    project(1)
    queries()
    side_partner(0)
    project(2)
    pass_on(2, 0)
    project(3)
    pass_on(2, 1)
    attend(0, 2, (0, 0), (1, 0))
    attend(2, 2, (0, 0), (1, 0))
    pass_on(2, 2)
    pass_on(3, 0)
    side(1)
    pass_on(2, 3)
    side_partner(1)
    project(4)
    pass_on(3, 1)
    project(5)
    attend(0, 2, (0, 1), (0, 2))
    pass_on(3, 2)
    attend(2, 2, (0, 1), (0, 2))
    pass_on(3, 3)
    pass_on(2, 4)
    attend(0, 2, (1, 1), (2, 0))
    attend(2, 2, (1, 1), (2, 0))
    pass_on(2, 5)
    landed(3, 0)
    landed(3, 1)
    attend(0, 2, (1, 2), (3, 0))
    attend(2, 2, (1, 2), (3, 0))
    far(0)
    far(1)
    pass_on(3, 4)
    arrive(hbuf.at[x_far, 0, other_core], HP + 6)
    project(6)
    arrive(hbuf.at[x_far, 1, other_core], HP + 7)
    project(7)
    pass_on(3, 5)
    attend(0, 2, (0, 3), (2, 1))
    attend(2, 2, (0, 3), (2, 1))
    landed(3, 2)
    landed(3, 4)
    attend(0, 2, (2, 2), (3, 1))
    pass_on(2, 6)
    attend(2, 2, (2, 2), (3, 1))
    pass_on(2, 7)
    landed(3, 3)
    landed(3, 5)
    attend(0, 2, (1, 3), (3, 2))
    attend(2, 2, (1, 3), (3, 2))
    pass_on(3, 6)
    pass_on(3, 7)
    attend(0, 4, (2, 3))
    landed(3, 6)
    landed(3, 7)

    here = out.at[:, pl.ds(pl.multiple_of(u * 2 * HD, HD), 2 * HD)]
    own_out = pltpu.make_async_copy(obuf.at[u], here, lsem.at[5])
    for offset in (2, 1, 3, 0):
        j = lax.rem(x + offset, 4)
        attend(j, 1, (3, 3))
        for head in range(2):
            place = 2 * j + head
            total = jnp.sum(l_ref[place], axis=0, keepdims=True)
            value = (acc_ref[place] / total).T.astype(jnp.bfloat16)
            obuf[pl.ds(2 * j, 2), :, head * HD : (head + 1) * HD] = value.reshape(2, 128, HD)
        if offset:
            for k, to in enumerate((core, other_core)):
                send(obuf.at[2 * j + to], here, OX + (offset - 1) * 2 + k, ul(2 * j + to))
        else:
            own_out.start()
            send(obuf.at[partner], here, OX + 6, ul(partner))
    own_out.wait()

    def out_from(index):
        return out.at[:, pl.ds(pl.multiple_of(index * 2 * HD, HD), 2 * HD)]

    for offset in (2, 1, 3):
        for k, source_core in enumerate((core, other_core)):
            arrive(out_from(2 * lax.rem(x + 4 - offset, 4) + source_core), OX + (offset - 1) * 2 + k)
    arrive(out_from(partner), OX + 6)
    for copy in sends:
        copy.wait_send()


def shards(hidden_in, queries, pair_weight, span_order, yarn_divisor):
    anywhere = pl.BlockSpec(memory_space=pl.ANY)
    hbm = pl.BlockSpec(memory_space=pltpu.HBM)
    out = pl.pallas_call(
        kernel,
        out_shape=jax.ShapeDtypeStruct((128, QH * HD), jnp.bfloat16),
        in_specs=[
            hbm, hbm, hbm, hbm, hbm,
        ],
        out_specs=anywhere,
        scratch_shapes=[
            pltpu.SMEM((1, 32), jnp.int32),
            pltpu.VMEM((1, HD // 2), jnp.int32),
            pltpu.VMEM((1024, HD), jnp.float32),
            pltpu.VMEM((1024, HD), jnp.float32),
            pltpu.VMEM((2, 2, NZ, 128, 2 * HD), jnp.bfloat16),
            pltpu.VMEM((4, 2, 2, 64, 4096), jnp.bfloat16),
            pltpu.VMEM((UL, 128, 2 * HD), jnp.bfloat16),
            pltpu.VMEM((8, 256, HD), jnp.bfloat16),
            pltpu.VMEM((STEPS + 1, 4, 2, 2, 128, HD), jnp.bfloat16),
            pltpu.VMEM((8, 1, 256), jnp.float32),
            pltpu.VMEM((8, 8, 256), jnp.float32),
            pltpu.VMEM((8, HD, 256), jnp.float32),
            pltpu.VMEM((UL, 128, 2 * HD), jnp.bfloat16),
            pltpu.VMEM((2, 256, 256), jnp.float32),
            pltpu.VMEM((2, 256, 256), jnp.float32),
            pltpu.VMEM((1, 256), jnp.float32),
            pltpu.VMEM((1, 256), jnp.float32),
            pltpu.SemaphoreType.DMA((104,)),
            pltpu.SemaphoreType.DMA((104,)),
            pltpu.SemaphoreType.DMA((8,)),
        ],
        compiler_params=pltpu.CompilerParams(
            collective_id=0, has_side_effects=True, vmem_limit_bytes=61900 * 1024
        ),
    )(span_order, yarn_divisor[None, :], hidden_in[0], queries[0], pair_weight)
    return out[None]


def solution(mesh):
    return jax.shard_map(
        shards,
        mesh=mesh,
        in_specs=(
            P("dp", ("blk", "ulysses"), None),
            P("dp", ("blk", "ulysses"), None),
            P(("dp", "blk"), None),
            P("dp", None),
            P(),
        ),
        out_specs=P("dp", ("blk", "ulysses"), None),
        check_vma=False,
    )
```

```python
import math

import jax
import jax.numpy as jnp
from jax import lax
from jax.experimental import pallas as pl
from jax.experimental.pallas import tpu as pltpu
from jax.sharding import PartitionSpec as P
import numpy as np

KVH = 8
HD = 128
QH = 16
STEPS = 3
UL = 8
NZ = 8
LOG_BASE = math.log(500000.0)
MESH = pl.DeviceIdType.MESH
SCALE2 = (1.0 / math.sqrt(HD)) * math.log2(math.e)
NEG = -1.0e30
FREQUENCIES = [
    float(np.exp(np.float32(-LOG_BASE) * (np.float32(2 * f) / np.float32(HD)), dtype=np.float32)) for f in range(HD // 2)
]
FAR = 2.0e30


def wrap(value, size):
    return lax.rem(value + size, size)


def kernel(
    order_hbm, divisor_hbm, hid, qry, pw, out,
    order_ref, divisor_ref, cos_ref, sin_ref, wk_ref, wv_ref, hbuf, qbuf, qrot, kvbuf, m_ref, l_ref, acc_ref, obuf,
    sa_ref, sb_ref, ta_ref, tb_ref, ssem, rsem, lsem,
):
    dp = lax.axis_index("dp")
    u = lax.axis_index("ulysses")
    blk = lax.axis_index("blk")
    core = lax.rem(u, 2)
    other_core = 1 - core
    x = u // 2
    yh = blk // NZ
    z = lax.rem(blk, NZ)
    y = yh * 2 + dp

    counter = [0]

    def take(n):
        base = counter[0]
        counter[0] += n
        return base

    def ul(index):
        return {"ulysses": index}

    def chip(offset, on_core):
        return ul(2 * lax.rem(x + offset, 4) + on_core)

    def ydev(offset):
        other = lax.rem(y + offset, 4)
        return {"dp": lax.rem(other, 2), "blk": (other // 2) * NZ + z}

    def zdev(offset):
        return {"blk": yh * NZ + wrap(z + offset, NZ)}

    x_plus, x_far, x_minus = lax.rem(x + 1, 4), lax.rem(x + 2, 4), lax.rem(x + 3, 4)
    partner = u + 1 - 2 * core
    next_blk = {"blk": lax.rem(blk + 1, 16)}
    prev_blk = {"blk": lax.rem(blk + 15, 16)}

    def rcopy(src, dst, index, device):
        return pltpu.make_async_remote_copy(
            src_ref=src, dst_ref=dst, send_sem=ssem.at[index], recv_sem=rsem.at[index],
            device_id=device, device_id_type=MESH,
        )

    sends = []

    def send(src, dst, index, device):
        copy = rcopy(src, dst, index, device)
        copy.start()
        sends.append(copy)

    def arrive(dst, index):
        rcopy(dst, dst, index, ul(partner)).wait_recv()

    own_k = pw.at[:, pl.ds(pl.multiple_of(u * HD, HD), HD)]
    own_v = pw.at[:, pl.ds(pl.multiple_of(KVH * HD + u * HD, HD), HD)]
    WB = (take(4), take(3))
    WAY = take(3)
    WAZ = (take(16), take(16))
    WBY = (take(8), take(8))
    WBF = take(8)
    HX, HR, HP = take(4), take(2), take(8)
    QX = take(7)
    KV = take(24)
    OX = take(7)

    def vpiece(yy, zz):
        return wv_ref.at[lax.rem(yy, 2), yy // 2, zz]

    def kpiece(yy, zz):
        return wk_ref.at[lax.rem(yy, 2), yy // 2, zz]

    def hid_half(a):
        return hid.at[pl.ds(a * 64, 64)]

    def qry_for(index):
        return qry.at[:, pl.ds(pl.multiple_of(index * 2 * HD, HD), 2 * HD)]

    local = [
        pltpu.make_async_copy(own_k, kpiece(y, z), lsem.at[0]),
        pltpu.make_async_copy(own_v, vpiece(y, z), lsem.at[1]),
        pltpu.make_async_copy(hid_half(0), hbuf.at[x, 0, core], lsem.at[2]),
        pltpu.make_async_copy(hid_half(1), hbuf.at[x, 1, core], lsem.at[3]),
        pltpu.make_async_copy(qry_for(u), qbuf.at[u], lsem.at[4]),
        pltpu.make_async_copy(order_hbm, order_ref, lsem.at[6]),
        pltpu.make_async_copy(divisor_hbm, divisor_ref, lsem.at[7]),
    ]
    for copy in local:
        copy.start()

    barrier = pltpu.get_barrier_semaphore()
    greet = [ul(lax.rem(u + o, UL)) for o in range(1, UL)]
    greet += [ydev(o) for o in range(1, 4)]
    greet += [zdev(1), zdev(-1), zdev(2), zdev(-2), next_blk, prev_blk]
    for device in greet:
        pl.semaphore_signal(barrier, inc=1, device_id=device, device_id_type=MESH)
    pl.semaphore_wait(barrier, len(greet))

    send(own_v, vpiece(y, z), WB[0], zdev(1))
    send(own_v, vpiece(y, z), WB[1], zdev(-1))
    send(own_v, vpiece(y, z), WB[0] + 1, zdev(2))
    send(own_v, vpiece(y, z), WB[1] + 1, zdev(-2))
    for o, spot in ((2, 2), (1, 0), (3, 1)):
        send(own_k, kpiece(y, z), WAY + spot, ydev(o))
    for a in range(2):
        send(hid_half(a), hbuf.at[x, a, core], HX + a, chip(1, core))
        send(hid_half(a), hbuf.at[x, a, core], HX + 2 + a, chip(3, core))
        send(hid_half(a), hbuf.at[x, a, core], HP + a, ul(partner))
        if a == 0:
            for o in range(1, UL):
                peer = lax.rem(u + o, UL)
                send(qry_for(peer), qbuf.at[u], QX + o - 1, ul(peer))

    spots = {0: 0, -1: 1, 1: 2, -2: 3, 2: 4, -3: 5, 3: 6, -4: 7}
    y_up, y_down, y_far = lax.rem(y + 1, 4), lax.rem(y + 3, 4), lax.rem(y + 2, 4)

    def v_spread(offset, source=None):
        zz = wrap(z + offset, NZ)
        src = vpiece(y, zz) if source is None else source
        send(src, vpiece(y, zz), WBY[0] + spots[offset], ydev(1))
        send(src, vpiece(y, zz), WBY[1] + spots[offset], ydev(3))

    def v_hop(h):
        for way, step in ((0, -1), (1, 1)):
            if h <= (4, 3)[way]:
                piece = vpiece(y, wrap(z + step * h, NZ))
                arrive(piece, WB[way] + h - 1)
                if h == 2:
                    send(piece, piece, WB[way] + 2, zdev(-step))
                    if way == 0:
                        send(piece, piece, WB[way] + 3, zdev(2))
                v_spread(step * h)

    def v_across(*offsets):
        for offset in offsets:
            zz = wrap(z + offset, NZ)
            spot = spots[offset]
            arrive(vpiece(y_down, zz), WBY[0] + spot)
            if spot % 2 == 0:
                send(vpiece(y_down, zz), vpiece(y_down, zz), WBF + spot, ydev(1))
            arrive(vpiece(y_up, zz), WBY[1] + spot)
            if spot % 2 == 1:
                send(vpiece(y_up, zz), vpiece(y_up, zz), WBF + spot, ydev(3))

    k_from = (y, y_down, y_up, y_far)
    k_last = ((4, 3), (4, 3), (3, 4), (3, 4))

    def k_start(p):
        if p:
            arrive(kpiece(k_from[p], z), WAY + p - 1)
        src = kpiece(k_from[p], z) if p else own_k
        for way, step in ((0, -1), (1, 1)):
            send(src, kpiece(k_from[p], z), WAZ[way] + 4 * p, zdev(-step))

    def k_hop(h, *which):
        for p in which:
            for way, step in ((0, -1), (1, 1)):
                if h <= k_last[p][way]:
                    piece = kpiece(k_from[p], wrap(z + step * h, NZ))
                    arrive(piece, WAZ[way] + 4 * p + h - 1)
                    if h < k_last[p][way]:
                        send(piece, piece, WAZ[way] + 4 * p + h, zdev(-step))

    def side(a):
        arrive(hbuf.at[x_minus, a, core], HX + a)
        if a == 1:
            send(hbuf.at[x_minus, 1, core], hbuf.at[x_minus, 1, core], HR + 1, chip(1, core))
        send(hbuf.at[x_minus, a, core], hbuf.at[x_minus, a, core], HP + 2 + a, ul(partner))
        arrive(hbuf.at[x_plus, a, core], HX + 2 + a)
        if a == 0:
            send(hbuf.at[x_plus, 0, core], hbuf.at[x_plus, 0, core], HR, chip(3, core))
        send(hbuf.at[x_plus, a, core], hbuf.at[x_plus, a, core], HP + 4 + a, ul(partner))

    k_start(0)
    v_spread(0, own_v)
    v_hop(1)
    k_start(1)
    k_start(2)
    v_hop(2)
    v_across(0)
    k_start(3)
    k_hop(1, 0)
    v_across(-1, 1)
    k_hop(1, 1, 2)
    v_hop(3)
    v_hop(4)
    k_hop(1, 3)
    v_across(-2, 2)
    k_hop(2, 0, 1, 2)
    v_across(-3, 3)
    k_hop(2, 3)
    k_hop(3, 0)
    v_across(-4)
    k_hop(3, 1, 2, 3)
    side(0)

    local[5].wait()
    local[6].wait()
    lane64 = lax.broadcasted_iota(jnp.int32, (1, HD // 2), 1)
    inverse = jnp.zeros((1, HD // 2), jnp.float32)
    for f, value in enumerate(FREQUENCIES):
        inverse = jnp.where(lane64 == f, value, inverse)
    inverse = inverse / divisor_ref[...].astype(jnp.float32)
    inverse = jnp.concatenate([inverse, inverse], axis=1)

    def table(i, carry):
        start = order_ref[0, 2 * blk + i // 4] * 512 + lax.rem(i, 4) * 128
        pos = lax.broadcasted_iota(jnp.int32, (128, HD), 0) + start
        angle = pos.astype(jnp.float32) * inverse
        lane = lax.broadcasted_iota(jnp.int32, (128, HD), 1)
        sine = jnp.sin(angle)
        at = pl.ds(pl.multiple_of(i * 128, 128), 128)
        cos_ref[at, :] = jnp.cos(angle)
        sin_ref[at, :] = jnp.where(lane < HD // 2, -sine, sine)
        return carry

    lax.fori_loop(0, UL, table, 0)
    m_ref[...] = jnp.full_like(m_ref, NEG)
    l_ref[...] = jnp.zeros_like(l_ref)
    acc_ref[...] = jnp.zeros_like(acc_ref)

    local[0].wait()
    k_hop(4, 0, 1, 2, 3)
    for offset in spots:
        arrive(vpiece(y_far, wrap(z + offset, NZ)), WBF + spots[offset])
    local[1].wait()

    chunk = (x, x + 1 - 2 * lax.rem(x, 2), 3 - x, x_far)
    pieces = ((0, 0), (0, 1), (1, 0), (2, 0), (1, 1), (2, 1), (3, 0), (3, 1))

    def project(n):
        xc, a = chunk[pieces[n][0]], pieces[n][1]
        rows = hbuf[xc, a].reshape(128, 4096)
        weight = jnp.concatenate([wk_ref[...].reshape(4096, HD), wv_ref[...].reshape(4096, HD)], axis=1)
        result = jnp.dot(rows, weight, preferred_element_type=jnp.float32)
        key = result[:, :HD]
        turned = pltpu.roll(key, HD // 2, 1)
        for k in range(2):
            at = pl.ds(pl.multiple_of(xc * 256 + k * 128 + a * 64, 64), 64)
            part = slice(k * 64, (k + 1) * 64)
            rope = key[part] * cos_ref[at, :] + turned[part] * sin_ref[at, :]
            kvbuf[0, xc, a, 0, part] = rope.astype(jnp.bfloat16)
        kvbuf[0, xc, a, 1] = result[:, HD:].T.astype(jnp.bfloat16)
        pass_on(1, n)

    def kv_region(d, n):
        return kvbuf.at[d, chunk[pieces[n][0]], pieces[n][1]]

    def landed(d, n):
        arrive(kv_region(d, n), KV + (d - 1) * 8 + n)

    def pass_on(d, n):
        if d > 1:
            landed(d - 1, n)
        send(kv_region(d - 1, n), kv_region(d, n), KV + (d - 1) * 8 + n, next_blk)

    def side_partner(a):
        arrive(hbuf.at[x_minus, a, other_core], HP + 2 + a)
        arrive(hbuf.at[x_plus, a, other_core], HP + 4 + a)


    def rope_slice(s, carry):
        at = pl.ds(pl.multiple_of(s * 128, 128), 128)
        cosine = cos_ref[at, :]
        sine = sin_ref[at, :]
        for head in range(2):
            q = qbuf[s, :, head * HD : (head + 1) * HD].astype(jnp.float32)
            q = q * cosine + pltpu.roll(q, HD // 2, 1) * sine
            place = (s // 2) * 2 + head
            qrot[place, pl.ds(pl.multiple_of(lax.rem(s, 2) * 128, 128), 128)] = q.astype(jnp.bfloat16)
        return carry

    def queries():
        local[4].wait()
        for o in range(1, UL):
            arrive(qbuf.at[lax.rem(u + UL - o, UL)], QX + o - 1)
        lax.fori_loop(0, UL, rope_slice, 0)

    def far(a):
        arrive(hbuf.at[x_far, a, core], HR + a)
        send(hbuf.at[x_far, a, core], hbuf.at[x_far, a, core], HP + 6 + a, ul(partner))

    def attend(first, count, *tiles):
        def shut(j, d, c):
            source = lax.rem(blk + 16 - d, 16)
            return order_ref[0, 2 * source + chunk[c] // 2] > order_ref[0, 2 * blk + j // 2]

        def measure(s_ref, top_ref, j, head):
            query = qrot[2 * j + head]
            top = None
            for t, (d, c) in enumerate(tiles):
                keys = kvbuf[d, chunk[c], :, 0].reshape(256, HD)
                score = lax.dot_general(
                    keys, query, (((1,), (1,)), ((), ())), preferred_element_type=jnp.float32
                )
                if d == 0:
                    row = lax.broadcasted_iota(jnp.int32, score.shape, 0)
                    shift = (lax.shift_right_logical(row, 6) & 1) - lax.shift_right_logical(row, 7)
                    key_at = row + 64 * shift + lax.rem(chunk[c], 2) * 256
                    apart = lax.rem(chunk[c] // 2 + j // 2, 2)
                    query_at = lax.broadcasted_iota(jnp.int32, score.shape, 1) + (
                        lax.rem(j, 2) * 256 + apart * 1024
                    )
                    score = jnp.where(query_at >= key_at, score, 4.0 * NEG)
                s_ref[t] = score
                here = jnp.max(score, axis=0, keepdims=True) + jnp.where(shut(j, d, c), -FAR, 0.0)
                top = here if top is None else jnp.maximum(top, here)
            top_ref[...] = top

        def gather(s_ref, top_ref, j, head):
            place = 2 * j + head
            old = m_ref[place]
            new = jnp.maximum(old, top_ref[...])
            shrink = jnp.exp2((old - new) * SCALE2)
            total = l_ref[place] * shrink
            mixed = acc_ref[place] * shrink
            for t, (d, c) in enumerate(tiles):
                base = new + jnp.where(shut(j, d, c), FAR, 0.0)
                weight = jnp.exp2((s_ref[t] - base) * SCALE2)
                total = total + jnp.sum(weight.reshape(32, 8, 256), axis=0)
                values = jnp.concatenate([kvbuf[d, chunk[c], 0, 1], kvbuf[d, chunk[c], 1, 1]], axis=1)
                mixed = mixed + jnp.dot(
                    values, weight.astype(jnp.bfloat16), preferred_element_type=jnp.float32
                )
            l_ref[place] = total
            acc_ref[place] = mixed
            m_ref[place] = new

        measure(sa_ref, ta_ref, first, 0)
        if count == 1:
            measure(sb_ref, tb_ref, first, 1)
            gather(sa_ref, ta_ref, first, 0)
            gather(sb_ref, tb_ref, first, 1)
            return

        def one_chip(i, carry):
            j = first + i
            measure(sb_ref, tb_ref, j, 1)
            gather(sa_ref, ta_ref, j, 0)
            measure(sa_ref, ta_ref, first + jnp.minimum(i + 1, count - 1), 0)
            gather(sb_ref, tb_ref, j, 1)
            return carry

        lax.fori_loop(0, count, one_chip, 0)

    local[2].wait()
    arrive(hbuf.at[x, 0, other_core], HP + 0)
    project(0)
    local[3].wait()
    arrive(hbuf.at[x, 1, other_core], HP + 1)
    project(1)
    queries()
    side_partner(0)
    project(2)
    project(3)
    pass_on(2, 0)
    pass_on(2, 1)
    attend(0, 2, (0, 0), (1, 0))
    attend(2, 2, (0, 0), (1, 0))
    pass_on(2, 2)
    pass_on(2, 3)
    side(1)
    pass_on(3, 0)
    side_partner(1)
    project(4)
    project(5)
    pass_on(3, 1)
    attend(0, 2, (0, 1), (0, 2))
    attend(2, 2, (0, 1), (0, 2))
    pass_on(3, 2)
    pass_on(3, 3)
    pass_on(2, 4)
    attend(0, 2, (1, 1), (2, 0))
    attend(2, 2, (1, 1), (2, 0))
    pass_on(2, 5)
    landed(3, 0)
    landed(3, 1)
    attend(0, 2, (1, 2), (3, 0))
    attend(2, 2, (1, 2), (3, 0))
    far(0)
    far(1)
    arrive(hbuf.at[x_far, 0, other_core], HP + 6)
    project(6)
    pass_on(3, 4)
    arrive(hbuf.at[x_far, 1, other_core], HP + 7)
    project(7)
    attend(0, 2, (0, 3), (2, 1))
    pass_on(3, 5)
    attend(2, 2, (0, 3), (2, 1))
    pass_on(2, 6)
    landed(3, 2)
    landed(3, 4)
    attend(0, 2, (2, 2), (3, 1))
    attend(2, 2, (2, 2), (3, 1))
    pass_on(2, 7)
    landed(3, 3)
    landed(3, 5)
    attend(0, 2, (1, 3), (3, 2))
    attend(2, 2, (1, 3), (3, 2))
    pass_on(3, 6)
    pass_on(3, 7)
    attend(0, 4, (2, 3))
    landed(3, 6)
    landed(3, 7)

    here = out.at[:, pl.ds(pl.multiple_of(u * 2 * HD, HD), 2 * HD)]
    own_out = pltpu.make_async_copy(obuf.at[u], here, lsem.at[5])
    for offset in (2, 1, 3, 0):
        j = lax.rem(x + offset, 4)
        attend(j, 1, (3, 3))
        for head in range(2):
            place = 2 * j + head
            total = jnp.sum(l_ref[place], axis=0, keepdims=True)
            value = (acc_ref[place] / total).T.astype(jnp.bfloat16)
            obuf[pl.ds(2 * j, 2), :, head * HD : (head + 1) * HD] = value.reshape(2, 128, HD)
        if offset:
            for k, to in enumerate((core, other_core)):
                send(obuf.at[2 * j + to], here, OX + (offset - 1) * 2 + k, ul(2 * j + to))
        else:
            own_out.start()
            send(obuf.at[partner], here, OX + 6, ul(partner))
    own_out.wait()

    def out_from(index):
        return out.at[:, pl.ds(pl.multiple_of(index * 2 * HD, HD), 2 * HD)]

    for offset in (2, 1, 3):
        for k, source_core in enumerate((core, other_core)):
            arrive(out_from(2 * lax.rem(x + 4 - offset, 4) + source_core), OX + (offset - 1) * 2 + k)
    arrive(out_from(partner), OX + 6)
    for copy in sends:
        copy.wait_send()


def shards(hidden_in, queries, pair_weight, span_order, yarn_divisor):
    anywhere = pl.BlockSpec(memory_space=pl.ANY)
    hbm = pl.BlockSpec(memory_space=pltpu.HBM)
    out = pl.pallas_call(
        kernel,
        out_shape=jax.ShapeDtypeStruct((128, QH * HD), jnp.bfloat16),
        in_specs=[
            hbm, hbm, hbm, hbm, hbm,
        ],
        out_specs=anywhere,
        scratch_shapes=[
            pltpu.SMEM((1, 32), jnp.int32),
            pltpu.VMEM((1, HD // 2), jnp.int32),
            pltpu.VMEM((1024, HD), jnp.float32),
            pltpu.VMEM((1024, HD), jnp.float32),
            pltpu.VMEM((2, 2, NZ, 128, HD), jnp.bfloat16),
            pltpu.VMEM((2, 2, NZ, 128, HD), jnp.bfloat16),
            pltpu.VMEM((4, 2, 2, 64, 4096), jnp.bfloat16),
            pltpu.VMEM((UL, 128, 2 * HD), jnp.bfloat16),
            pltpu.VMEM((8, 256, HD), jnp.bfloat16),
            pltpu.VMEM((STEPS + 1, 4, 2, 2, 128, HD), jnp.bfloat16),
            pltpu.VMEM((8, 1, 256), jnp.float32),
            pltpu.VMEM((8, 8, 256), jnp.float32),
            pltpu.VMEM((8, HD, 256), jnp.float32),
            pltpu.VMEM((UL, 128, 2 * HD), jnp.bfloat16),
            pltpu.VMEM((2, 256, 256), jnp.float32),
            pltpu.VMEM((2, 256, 256), jnp.float32),
            pltpu.VMEM((1, 256), jnp.float32),
            pltpu.VMEM((1, 256), jnp.float32),
            pltpu.SemaphoreType.DMA((120,)),
            pltpu.SemaphoreType.DMA((120,)),
            pltpu.SemaphoreType.DMA((8,)),
        ],
        compiler_params=pltpu.CompilerParams(
            collective_id=0, has_side_effects=True, vmem_limit_bytes=61900 * 1024
        ),
    )(span_order, yarn_divisor[None, :], hidden_in[0], queries[0], pair_weight)
    return out[None]


def solution(mesh):
    return jax.shard_map(
        shards,
        mesh=mesh,
        in_specs=(
            P("dp", ("blk", "ulysses"), None),
            P("dp", ("blk", "ulysses"), None),
            P(("dp", "blk"), None),
            P("dp", None),
            P(),
        ),
        out_specs=P("dp", ("blk", "ulysses"), None),
        check_vma=False,
    )
```
